256 devices in a mesh: cuts: 2 (over core), tile: 128 (over z, y, x).
Axes of the slice: x: 4, y: 4, z: 8, core: 2. Of those that a mesh axis runs over, the one named last changes fastest.
Arguments:
- transmission: float32 [2, 2, 32768, 512], P(None, 'cuts', 'tile')
- illumination: float32 [2, 256, 256], replicated, may hold values from -6 to 6
- measured: float32 [128, 256, 256], P('tile'), may hold values from 0.2 to 5
- offsets: int32 [128, 2], P('tile'), may hold values from 0 to 256, as said below
- live_count: int32 [128], P('tile'), may hold values from 1 to 1, as said below
Outputs:
- object_grad: float32 [2, 2, 32768, 512], P(None, 'cuts', 'tile')
The draws below stay inside these ranges and needn't reach their ends.
Inputs may be any that keep to these rules, and one draw needn't show every extreme that they name: offsets[j, 0] counts rows from the first row of tile j // 1 and may run past that tile's end (past the last tile, into the first); offsets[j, 1] counts columns; in every draw some live slot has row 255 and column 256. `live_count`: slots of a tile at or beyond its count are unused; some tile has all 1 slots used in every draw.
All inputs are finite; a program needn't handle non-finite values.
Results may differ from the reference program's by a relative error of at most 0.0049.
Values may be sent and summed in bfloat16 or wider, within the bound.
No kernel may reach another device: no remote copies, remote signals or barrier semaphores. Data moves between devices by JAX's collectives and lax.ppermute only.
A program may use at most 64 MiB of HBM per device.

```python
import math
import jax
import jax.numpy as jnp
from jax import lax

PW = 256
S_DEV = 1
TY = 256
WX = 512
P_DEV = 1
SLICES = 2
NY = 32768
PROBES = 128
N_TILE = 128


def draw_transmission(key, part):
    key_amp, key_phase = jax.random.split(jax.random.fold_in(key, 11))
    shape = (SLICES, NY, WX)
    amplitude = 1.0 + 0.1 * jax.random.normal(key_amp, shape, jnp.float32)
    phase = 0.35 * jax.random.normal(key_phase, shape, jnp.float32)
    return jnp.stack([amplitude * jnp.cos(phase), amplitude * jnp.sin(phase)], axis=0).astype(jnp.float32)


def draw_offsets(key, part):
    keys = jax.random.split(jax.random.fold_in(key, 23), 4)
    row_values = jax.random.randint(keys[0], (PROBES,), 0, TY)
    col_values = jax.random.randint(keys[1], (PROBES,), 0, WX - PW + 1)
    high_tile = jax.random.randint(keys[2], (), 0, N_TILE)
    low_tile = (high_tile + 1 + jax.random.randint(keys[3], (), 0, max(N_TILE - 1, 1))) % N_TILE
    row_values = row_values.at[high_tile * P_DEV].set(TY - 1).at[low_tile * P_DEV].set(0)
    col_values = col_values.at[high_tile * P_DEV].set(WX - PW).at[low_tile * P_DEV].set(0)
    return jnp.stack([row_values, col_values], axis=1).astype(jnp.int32)


def draw_live_count(key, part):
    keys = jax.random.split(jax.random.fold_in(key, 37), 2)
    counts = jax.random.randint(keys[0], (N_TILE,), 1, P_DEV + 1)
    full_tile = jax.random.randint(keys[1], (), 0, N_TILE)
    return counts.at[full_tile].set(P_DEV).astype(jnp.int32)


def shard_levels(rng, extent, cuts, smallest, high):
    def one(dim, parts):
        steps = jax.random.uniform(jax.random.fold_in(jax.random.fold_in(rng, 6), dim), (parts,), jnp.float32, smallest / len(cuts), high / len(cuts))
        return jnp.repeat(jnp.exp(steps), extent[dim] // parts).reshape((-1,) + (1,) * (len(extent) - dim - 1))

    level = one(*cuts[0])
    for cut in cuts[1:]:
        level = level * one(*cut)
    return level


def gaussian(rng, dims, scale, reach, held_as=jnp.bfloat16):
    entries = jax.random.normal(rng, dims, jnp.float32) * scale
    return jnp.minimum(jnp.maximum(entries, -reach), reach).astype(held_as)


def setup_inputs(seed: int = 0) -> dict:
    streams_of = jax.random.split(jax.random.key(seed), 6)
    return {
        "transmission": draw_transmission(jax.random.fold_in(streams_of[5], 71), 0),
        "illumination": gaussian(streams_of[1], (2, PW, PW), 0.7, 6.0, jnp.float32),
        "measured": jnp.clip(jnp.exp(math.log(5.0) - 3.218876 * jax.random.uniform(streams_of[2], (PROBES, PW, PW), jnp.float32) ** shard_levels(streams_of[2], (PROBES, PW, PW), ((0, 128),), -0.2, 0.2)), 0.2, 5.0),
        "offsets": draw_offsets(jax.random.fold_in(streams_of[5], 71), 0),
        "live_count": draw_live_count(jax.random.fold_in(streams_of[5], 71), 0),
    }


def fresnel_tables(patch_width):
    freq = jnp.arange(patch_width, dtype=jnp.int32)
    signed = jnp.where(freq < patch_width // 2, freq, freq - patch_width).astype(jnp.float32)
    phases = math.pi * signed * signed / (4.0 * patch_width)
    product = freq[:, None] * freq[None, :] % patch_width
    angles = 2.0 * math.pi * product.astype(jnp.float32) / patch_width
    cos_table = jnp.cos(angles)
    sin_table = jnp.sin(angles)
    shifted_real = jnp.cos(angles - phases[None, :])
    shifted_imag = jnp.sin(angles - phases[None, :])
    highest = lax.Precision.HIGHEST
    prop_real = (jnp.dot(shifted_real, cos_table, precision=highest) + jnp.dot(shifted_imag, sin_table, precision=highest)) / patch_width
    prop_imag = (jnp.dot(shifted_imag, cos_table, precision=highest) - jnp.dot(shifted_real, sin_table, precision=highest)) / patch_width
    factor = 1.0 / math.sqrt(patch_width)
    far_real = cos_table * factor
    far_imag = -sin_table * factor
    return (prop_real, prop_imag, far_real, far_imag)

def left_product(mat_real, mat_imag, real_part, imag_part):
    width = mat_real.shape[0]
    stacked = jnp.concatenate([jnp.concatenate([mat_real, -mat_imag], axis=1), jnp.concatenate([mat_imag, mat_real], axis=1)], axis=0)
    values = jnp.concatenate([real_part, imag_part], axis=-2)
    result = jnp.einsum('ab,...bc->...ac', stacked, values, precision=lax.Precision.HIGHEST)
    return (result[..., :width, :], result[..., width:, :])

def right_product(real_part, imag_part, mat_real, mat_imag):
    width = mat_real.shape[1]
    stacked = jnp.concatenate([jnp.concatenate([mat_real, mat_imag], axis=1), jnp.concatenate([-mat_imag, mat_real], axis=1)], axis=0)
    values = jnp.concatenate([real_part, imag_part], axis=-1)
    result = jnp.einsum('...ab,bc->...ac', values, stacked, precision=lax.Precision.HIGHEST)
    return (result[..., :width], result[..., width:])

def apply_forward(mat_real, mat_imag, real_part, imag_part):
    left_real, left_imag = left_product(mat_real, mat_imag, real_part, imag_part)
    return right_product(left_real, left_imag, mat_real.T, mat_imag.T)

def apply_adjoint(mat_real, mat_imag, real_part, imag_part):
    left_real, left_imag = left_product(mat_real.T, -mat_imag.T, real_part, imag_part)
    return right_product(left_real, left_imag, mat_real, -mat_imag)

def complex_times(first_real, first_imag, second_real, second_imag):
    return (first_real * second_real - first_imag * second_imag, first_real * second_imag + first_imag * second_real)

def conj_times(first_real, first_imag, second_real, second_imag):
    return (first_real * second_real + first_imag * second_imag, first_real * second_imag - first_imag * second_real)

def to_half(values):
    rounded = lax.optimization_barrier(values.astype(jnp.bfloat16))
    return rounded.astype(jnp.float32)

def one_probe(patch, illumination, target, flag, tables):
    prop_real, prop_imag, far_real, far_imag = tables
    wave_real = illumination[0]
    wave_imag = illumination[1]
    saved_waves = []
    for layer_index in range(SLICES):
        if layer_index > 0 and layer_index % S_DEV == 0:
            wave_real = to_half(wave_real)
            wave_imag = to_half(wave_imag)
        saved_waves.append((wave_real, wave_imag))
        chi_real, chi_imag = complex_times(wave_real, wave_imag, patch[0, layer_index], patch[1, layer_index])
        wave_real, wave_imag = apply_forward(prop_real, prop_imag, chi_real, chi_imag)
    out_real, out_imag = apply_forward(far_real, far_imag, wave_real, wave_imag)
    weight = (out_real * out_real + out_imag * out_imag - target) * flag
    grad_real, grad_imag = apply_adjoint(far_real, far_imag, weight * out_real, weight * out_imag)
    pieces = [None] * SLICES
    for layer_index in reversed(range(SLICES)):
        chi_real, chi_imag = apply_adjoint(prop_real, prop_imag, grad_real, grad_imag)
        kept_real, kept_imag = saved_waves[layer_index]
        pieces[layer_index] = jnp.stack(conj_times(kept_real, kept_imag, chi_real, chi_imag), axis=0)
        grad_real, grad_imag = conj_times(patch[0, layer_index], patch[1, layer_index], chi_real, chi_imag)
        if layer_index > 0 and layer_index % S_DEV == 0:
            grad_real = to_half(grad_real)
            grad_imag = to_half(grad_imag)
    return jnp.stack(pieces, axis=1)

def reference(transmission, illumination, measured, offsets, live_count):
    tables = fresnel_tables(PW)
    extended = jnp.concatenate([transmission, transmission[:, :, :PW, :]], axis=2)
    slot_index = jnp.arange(PROBES, dtype=jnp.int32)
    owner = slot_index // P_DEV
    live_flags = (slot_index % P_DEV < live_count[owner]).astype(jnp.float32)
    row_starts = (owner * TY + offsets[:, 0]).astype(jnp.int32)
    col_starts = offsets[:, 1].astype(jnp.int32)
    anchor = jnp.zeros((), jnp.int32)

    def add_probe(total, item):
        row_start, col_start, target, flag = item
        corner = (anchor, anchor, row_start, col_start)
        patch = lax.dynamic_slice(extended, corner, (2, SLICES, PW, PW))
        piece = one_probe(patch, illumination, target, flag, tables)
        current = lax.dynamic_slice(total, corner, (2, SLICES, PW, PW))
        return (lax.dynamic_update_slice(total, current + piece, corner), None)
    total, _ = lax.scan(add_probe, jnp.zeros_like(extended), (row_starts, col_starts, measured, live_flags))
    return total[:, :, :NY].at[:, :, :PW].add(total[:, :, NY:])
```

```python
import functools
import math

import jax
import jax.numpy as jnp
import numpy as np
from jax import lax
from jax.experimental import pallas as pl
from jax.experimental.pallas import tpu as pltpu
from jax.sharding import PartitionSpec as P

W = 256
HEAD = 16
TOP = 32000.0
MEASURED_STEP = 5.0 / TOP
VMEM = pl.BlockSpec(memory_space=pltpu.VMEM)
SMEM = pl.BlockSpec(memory_space=pltpu.SMEM)


def split_table(matrix):
    parts = []
    for factor in (matrix.real, matrix.imag - matrix.real, matrix.real + matrix.imag):
        factor = np.asarray(factor, np.float32)
        high = factor.astype(jnp.bfloat16)
        low = (factor - high.astype(np.float32)).astype(jnp.bfloat16)
        parts += [high, low]
    return np.stack(parts)


@functools.lru_cache(None)
def tables():
    freq = np.arange(W)
    signed = np.where(freq < W // 2, freq, freq - W).astype(np.float64)
    phase = np.pi * signed * signed / (4 * W)
    basis = np.exp(2j * np.pi * ((freq[:, None] * freq[None, :]) % W) / W)
    prop = (basis * np.exp(-1j * phase)[None, :]) @ np.conj(basis).T / W
    far = np.conj(basis) / math.sqrt(W)
    return split_table(prop), split_table(far)


def halves(value):
    high = value.astype(jnp.bfloat16)
    low = (value - high.astype(jnp.float32)).astype(jnp.bfloat16)
    return high, low


def dot(first, second):
    return jnp.dot(first, second, preferred_element_type=jnp.float32)


def right(value, table, which):
    high, low = halves(value)
    big, small = table[2 * which], table[2 * which + 1]
    return dot(high, big) + dot(low, big) + dot(high, small)


def left(value, table, which):
    high, low = halves(value)
    big, small = table[2 * which], table[2 * which + 1]
    return dot(big, high) + dot(big, low) + dot(small, high)


def product(times, real, imag, table, conj):
    both = times(real + imag, table, 0)
    if conj:
        return both + times(imag, table, 1), both - times(real, table, 2)
    return both - times(imag, table, 2), both + times(real, table, 1)


def transform(real, imag, table, conj):
    real, imag = product(right, real, imag, table, conj)
    return product(left, real, imag, table, conj)


def iota(dim):
    return lax.broadcasted_iota(jnp.int32, (W, W), dim)


def windowed(full, part, col):
    return jnp.where(iota(1) >= col, full[part, :, :W], full[part, :, W:])


def encode_kernel(offsets, own, measured, coded, coded_measured):
    col = offsets[0, 1]
    real = windowed(own.at[:, 0], 0, col)
    imag = windowed(own.at[:, 0], 1, col)
    peak = jnp.max(jnp.maximum(jnp.abs(real), jnp.abs(imag)), axis=0, keepdims=True)
    peak = jnp.max(peak, axis=1, keepdims=True)
    peak = jnp.broadcast_to(jnp.maximum(peak, 1e-30), (1, W))
    power = jnp.ceil(jnp.log(peak) * (1.0 / math.log(2.0)))
    gain = jnp.exp2(-power) * TOP
    coded[0, :W, :] = jnp.round(real * gain).astype(jnp.int32).astype(jnp.int16)
    coded[1, :W, :] = jnp.round(imag * gain).astype(jnp.int32).astype(jnp.int16)
    head = jnp.broadcast_to(power.astype(jnp.int32), (HEAD, W)).astype(jnp.int16)
    coded[0, W:, :] = head
    coded[1, W:, :] = head
    scaled = jnp.round(measured[0] * (1.0 / MEASURED_STEP))
    coded_measured[...] = scaled.astype(jnp.int32).astype(jnp.int16)


def decoded(coded, part):
    power = coded[0, W : W + HEAD, :].astype(jnp.int32).astype(jnp.float32)[0:1]
    step = jnp.exp2(power) * (1.0 / TOP)
    return coded[part, :W, :].astype(jnp.int32).astype(jnp.float32) * step


def patch_of(coded, own, row, col, part):
    return jnp.where(iota(0) >= row, decoded(coded, part), windowed(own, part, col))


def roll_kernel(offsets, illumination, rolled):
    row = lax.rem(offsets[0, 0], W)
    col = lax.rem(offsets[0, 1], W)
    for part in range(2):
        rolled[part] = pltpu.roll(pltpu.roll(illumination[part], row, 0), col, 1)


def first_kernel(offsets, coded, own, rolled, prop, psi):
    row, col = offsets[0, 0], offsets[0, 1]
    patch_real = patch_of(coded, own.at[:, 0], row, col, 0)
    patch_imag = patch_of(coded, own.at[:, 0], row, col, 1)
    wave_real, wave_imag = rolled[0], rolled[1]
    chi_real = wave_real * patch_real - wave_imag * patch_imag
    chi_imag = wave_real * patch_imag + wave_imag * patch_real
    out_real, out_imag = transform(chi_real, chi_imag, prop, False)
    psi[0] = out_real.astype(jnp.bfloat16)
    psi[1] = out_imag.astype(jnp.bfloat16)


def second_kernel(offsets, coded, other, psi, far, patch, field):
    row, col = offsets[0, 0], offsets[0, 1]
    patch_real = patch_of(coded, other, row, col, 0)
    patch_imag = patch_of(coded, other, row, col, 1)
    patch[0] = patch_real
    patch[1] = patch_imag
    wave_real, wave_imag = psi[0].astype(jnp.float32), psi[1].astype(jnp.float32)
    chi_real = wave_real * patch_real - wave_imag * patch_imag
    chi_imag = wave_real * patch_imag + wave_imag * patch_real
    out_real, out_imag = transform(chi_real, chi_imag, far, False)
    field[0] = out_real
    field[1] = out_imag


def third_kernel(live, coded_measured, field, psi, patch, far, grad, wave_grad):
    flag = (live[0] > 0).astype(jnp.float32)
    target = coded_measured[...].astype(jnp.int32).astype(jnp.float32) * MEASURED_STEP
    real, imag = field[0], field[1]
    weight = (real * real + imag * imag - target) * flag
    real, imag = transform(weight * real, weight * imag, far, True)
    wave_real, wave_imag = psi[0].astype(jnp.float32), psi[1].astype(jnp.float32)
    grad[0] = (wave_real * real + wave_imag * imag).astype(jnp.bfloat16)
    grad[1] = (wave_real * imag - wave_imag * real).astype(jnp.bfloat16)
    patch_real, patch_imag = patch[0], patch[1]
    wave_grad[0] = (patch_real * real + patch_imag * imag).astype(jnp.bfloat16)
    wave_grad[1] = (patch_real * imag - patch_imag * real).astype(jnp.bfloat16)


def fourth_kernel(wave_grad, rolled, prop, grad):
    real, imag = transform(wave_grad[0].astype(jnp.float32), wave_grad[1].astype(jnp.float32), prop, True)
    wave_real, wave_imag = rolled[0], rolled[1]
    grad[0] = (wave_real * real + wave_imag * imag).astype(jnp.bfloat16)
    grad[1] = (wave_real * imag - wave_imag * real).astype(jnp.bfloat16)


def place_kernel(offsets, before, core, own_first, own_second, spill_first, spill_second, out):
    row, col = offsets[0, 0], offsets[0, 1]
    row_before, col_before = before[0, 0], before[0, 1]

    def place(own, spill):
        for part in range(2):
            mine = jnp.where(iota(0) >= row, own[part].astype(jnp.float32), 0.0)
            theirs = jnp.where(iota(0) < row_before, spill[part].astype(jnp.float32), 0.0)
            out[part, 0, :, :W] = jnp.where(iota(1) >= col, mine, 0.0) + jnp.where(iota(1) >= col_before, theirs, 0.0)
            out[part, 0, :, W:] = jnp.where(iota(1) < col, mine, 0.0) + jnp.where(iota(1) < col_before, theirs, 0.0)

    @pl.when(core[0] == 0)
    def _():
        place(own_first, spill_first)

    @pl.when(core[0] != 0)
    def _():
        place(own_second, spill_second)


def call(kernel, outs, specs, name, mib=16):
    return pl.pallas_call(
        kernel,
        out_shape=outs,
        in_specs=specs,
        out_specs=jax.tree.map(lambda _: VMEM, outs),
        name=name,
        compiler_params=pltpu.CompilerParams(vmem_limit_bytes=mib << 20),
    )


def shaped(shape, dtype):
    return jax.ShapeDtypeStruct(shape, dtype)


def on_device(transmission, illumination, measured, offsets, live_count):
    prop, far = (jnp.asarray(t) for t in tables())
    count = lax.axis_size("tile")
    core = lax.axis_index("cuts").astype(jnp.int32)[None]
    axes = ("cuts", "tile")

    def hop(value, source, target, steps):
        pairs = [(source * count + k, target * count + (k + steps) % count) for k in range(count)]
        return lax.ppermute(value, axes, pairs)

    def both(value, steps):
        return lax.ppermute(value, "tile", [(k, (k + steps) % count) for k in range(count)])

    before = both(offsets, 1)
    live = both(live_count, 1)
    coded, coded_measured = call(
        encode_kernel,
        (shaped((2, W + HEAD, W), jnp.int16), shaped((W, W), jnp.int16)),
        [SMEM, VMEM, VMEM],
        "encode",
    )(offsets, transmission, measured)
    first_coded = hop(coded, 0, 0, 1)
    other = hop(transmission[:, 0], 1, 0, 0)
    second_coded = hop(coded, 1, 0, 1)
    target = hop(coded_measured, 1, 0, 1)
    rolled = call(roll_kernel, shaped((2, W, W), jnp.float32), [SMEM, VMEM], "roll")(before, illumination)
    psi = call(
        first_kernel, shaped((2, W, W), jnp.bfloat16), [SMEM, VMEM, VMEM, VMEM, VMEM], "first"
    )(before, first_coded, transmission, rolled, prop)
    patch, field = call(
        second_kernel,
        (shaped((2, W, W), jnp.float32), shaped((2, W, W), jnp.float32)),
        [SMEM, VMEM, VMEM, VMEM, VMEM],
        "second",
    )(before, second_coded, other, psi, far)
    grad_second, wave_grad = call(
        third_kernel,
        (shaped((2, W, W), jnp.bfloat16), shaped((2, W, W), jnp.bfloat16)),
        [SMEM, VMEM, VMEM, VMEM, VMEM, VMEM],
        "third",
    )(live, target, field, psi, patch, far)
    own_second = hop(grad_second, 0, 1, -1)
    spill_second = hop(grad_second, 0, 1, 0)
    grad_first = call(fourth_kernel, shaped((2, W, W), jnp.bfloat16), [VMEM, VMEM, VMEM], "fourth")(
        wave_grad, rolled, prop
    )
    own_first = hop(grad_first, 0, 0, -1)
    return call(
        place_kernel,
        shaped(transmission.shape, jnp.float32),
        [SMEM, SMEM, SMEM, VMEM, VMEM, VMEM, VMEM],
        "place",
    )(offsets, before, core, own_first, own_second, grad_first, spill_second)


def solution(mesh):
    placed = (P(None, "cuts", "tile", None), P(), P("tile", None, None), P("tile", None), P("tile"))
    return jax.shard_map(
        on_device,
        mesh=mesh,
        in_specs=placed,
        out_specs=P(None, "cuts", "tile", None),
        check_vma=False,
    )
```

```python
import functools
import math

import jax
import jax.numpy as jnp
import numpy as np
from jax import lax
from jax.experimental import pallas as pl
from jax.experimental.pallas import tpu as pltpu
from jax.sharding import PartitionSpec as P


W = 256
HEAD = 16
TOP = 32000.0
STEP = 32
ASIDE = 16
FLUSH = 64
MEASURED_STEP = 5.0 / TOP
VMEM = pl.BlockSpec(memory_space=pltpu.VMEM)
ANY = pl.BlockSpec(memory_space=pl.ANY)
SMEM = pl.BlockSpec(memory_space=pltpu.SMEM)


def split_table(matrix):
    parts = []
    for factor in (matrix.real, matrix.imag - matrix.real, matrix.real + matrix.imag):
        factor = np.asarray(factor, np.float32)
        high = factor.astype(jnp.bfloat16)
        low = (factor - high.astype(np.float32)).astype(jnp.bfloat16)
        parts += [high, low]
    return np.stack(parts)


@functools.lru_cache(None)
def tables():
    freq = np.arange(W)
    signed = np.where(freq < W // 2, freq, freq - W).astype(np.float64)
    phase = np.pi * signed * signed / (4 * W)
    basis = np.exp(2j * np.pi * ((freq[:, None] * freq[None, :]) % W) / W)
    prop = (basis * np.exp(-1j * phase)[None, :]) @ np.conj(basis).T / W
    far = np.conj(basis) / math.sqrt(W)
    return split_table(prop), split_table(far)


def halves(value):
    high = value.astype(jnp.bfloat16)
    low = (value - high.astype(jnp.float32)).astype(jnp.bfloat16)
    return high, low


def dot(first, second):
    return jnp.dot(first, second, preferred_element_type=jnp.float32)


def right(value, table, which):
    high, low = halves(value)
    big, small = table[2 * which], table[2 * which + 1]
    return dot(high, big) + dot(low, big) + dot(high, small)


def left(value, table, which):
    high, low = halves(value)
    big, small = table[2 * which], table[2 * which + 1]
    return dot(big, high) + dot(big, low) + dot(small, high)


def product(times, real, imag, table, conj):
    both = times(real + imag, table, 0)
    if conj:
        return both + times(imag, table, 1), both - times(real, table, 2)
    return both - times(imag, table, 2), both + times(real, table, 1)


def transform(real, imag, table, conj):
    real, imag = product(right, real, imag, table, conj)
    return product(left, real, imag, table, conj)


def iota(dim):
    return lax.broadcasted_iota(jnp.int32, (STEP, W), dim)


def windowed(full, part, rows, col):
    return jnp.where(iota(1) >= col, full[part, rows, :W], full[part, rows, W:])


def encode_kernel(offsets, live, own, coded):
    col = offsets[0, 1]
    held = own.at[:, 0]
    peak = jnp.zeros((8, W), jnp.float32)
    for start in range(0, W, STEP):
        rows = pl.ds(start, STEP)
        real, imag = windowed(held, 0, rows, col), windowed(held, 1, rows, col)
        high = jnp.maximum(jnp.abs(real), jnp.abs(imag))
        for piece in range(0, STEP, 8):
            peak = jnp.maximum(peak, high[piece : piece + 8])
    peak = jnp.max(jnp.max(peak, axis=1, keepdims=True), axis=0, keepdims=True)
    peak = jnp.broadcast_to(jnp.maximum(peak, 1e-30), (1, W))
    power = jnp.ceil(jnp.log(peak) * (1.0 / math.log(2.0)))
    gain = jnp.exp2(-power) * TOP
    for part in range(2):
        for start in range(0, W, STEP):
            rows = pl.ds(start, STEP)
            scaled = jnp.round(windowed(held, part, rows, col) * gain)
            coded[part, rows, :] = scaled.astype(jnp.int32).astype(jnp.int16)
    flag = jnp.where(live[0] > 0, 1, 0)
    coded[0, pl.ds(W, HEAD), :] = jnp.broadcast_to(power.astype(jnp.int32), (HEAD, W)).astype(jnp.int16)
    coded[1, pl.ds(W, HEAD), :] = jnp.full((HEAD, W), flag, jnp.int32).astype(jnp.int16)


def mixed_kernel(before, core, live, own, measured, coded, mixed):
    encode_kernel(before, live, own, coded)

    @pl.when(core[0] == 0)
    def _():
        for start in range(0, W, STEP):
            rows = pl.ds(start, STEP)
            scaled = jnp.round(measured[0, rows, :] * (1.0 / MEASURED_STEP))
            mixed[0, rows, :] = scaled.astype(jnp.int32).astype(jnp.int16)

    @pl.when(core[0] != 0)
    def _():
        mixed[...] = coded[...]


def head_of(coded, part):
    return coded[part, pl.ds(W, HEAD), :].astype(jnp.int32).astype(jnp.float32)[0:1]


def gain_of(coded):
    return jnp.exp2(head_of(coded, 0)) * (1.0 / TOP)


def decoded(coded, part, rows, gain):
    return coded[part, rows, :].astype(jnp.int32).astype(jnp.float32) * gain


def roll_kernel(offsets, before, core, illumination, rolled):
    row = lax.rem(jnp.where(core[0] == 0, before[0, 0], offsets[0, 0]), W)
    col = lax.rem(jnp.where(core[0] == 0, before[0, 1], offsets[0, 1]), W)
    for part in range(2):
        rolled[part] = pltpu.roll(pltpu.roll(illumination[part], row, 0), col, 1)


def times_patch(wave, patch, out):
    for start in range(0, W, STEP):
        rows = pl.ds(start, STEP)
        wave_real, wave_imag = wave[0, rows, :].astype(jnp.float32), wave[1, rows, :].astype(jnp.float32)
        patch_real, patch_imag = patch(0, rows, start), patch(1, rows, start)
        out[0, rows, :] = wave_real * patch_real - wave_imag * patch_imag
        out[1, rows, :] = wave_real * patch_imag + wave_imag * patch_real


def chosen(row, upper, lower):
    return lambda part, rows, start: jnp.where(
        start + iota(0) >= row, lower(part, rows), upper(part, rows)
    )


def first_slice(rolled, patch, prop, psi, chi):
    times_patch(rolled, patch, chi)
    out_real, out_imag = transform(chi[0], chi[1], prop, False)
    psi[0] = out_real.astype(jnp.bfloat16)
    psi[1] = out_imag.astype(jnp.bfloat16)


def first_kernel(offsets, before, core, direct, own, rolled, prop, psi, chi):
    @pl.when(core[0] == 0)
    def _():
        gain = gain_of(direct)
        local = own.at[:, 0]
        patch = chosen(
            before[0, 0],
            lambda part, rows: windowed(local, part, rows, before[0, 1]),
            lambda part, rows: decoded(direct, part, rows, gain),
        )
        first_slice(rolled, patch, prop, psi, chi)


def keeping(given, patch):
    def kept(part, rows, start):
        value = given(part, rows, start)
        patch[part, rows, :] = value
        return value

    return kept


def second_slice(given, psi, far, patch, field, chi):
    times_patch(psi, keeping(given, patch), chi)
    out_real, out_imag = transform(chi[0], chi[1], far, False)
    field[0] = out_real
    field[1] = out_imag


def second_kernel(offsets, before, core, crossed, edge, rolled, early, prop, far, psi, patch, field, chi):
    row = jnp.where(core[0] == 0, before[0, 0], offsets[0, 0])
    gain_crossed, gain_edge = gain_of(crossed), gain_of(edge)
    given = chosen(
        row,
        lambda part, rows: decoded(edge, part, rows, gain_edge),
        lambda part, rows: decoded(crossed, part, rows, gain_crossed),
    )

    @pl.when(core[0] == 0)
    def _():
        psi[...] = early[...]
        second_slice(given, psi, far, patch, field, chi)

    @pl.when(core[0] != 0)
    def _():
        first_slice(rolled, given, prop, psi, chi)


def late_kernel(offsets, core, border, own, psi, far, patch, field, chi):
    @pl.when(core[0] != 0)
    def _():
        gain_border = gain_of(border)
        local = own.at[:, 0]
        last = chosen(
            offsets[0, 0],
            lambda part, rows: decoded(border, part, rows, gain_border),
            lambda part, rows: windowed(local, part, rows, offsets[0, 1]),
        )
        second_slice(last, psi, far, patch, field, chi)


def conj_times(first, real, imag, out):
    for start in range(0, W, STEP):
        rows = pl.ds(start, STEP)
        keep = slice(start, start + STEP)
        first_real, first_imag = first[0, rows, :].astype(jnp.float32), first[1, rows, :].astype(jnp.float32)
        out[0, rows, :] = (first_real * real[keep] + first_imag * imag[keep]).astype(out.dtype)
        out[1, rows, :] = (first_real * imag[keep] - first_imag * real[keep]).astype(out.dtype)


def third_kernel(
    core, live, direct, border, measured, field, late_field, psi, patch, late_patch, rolled, prop, far, send, stay, chi, half
):
    def residue(field, target, alive):
        for start in range(0, W, STEP):
            rows = pl.ds(start, STEP)
            real, imag = field[0, rows, :], field[1, rows, :]
            weight = (real * real + imag * imag - target(rows)) * alive
            chi[0, rows, :] = weight * real
            chi[1, rows, :] = weight * imag

    @pl.when(core[0] == 0)
    def _():
        head = head_of(direct, 1)
        residue(field, lambda rows: border[0, rows, :].astype(jnp.int32).astype(jnp.float32) * MEASURED_STEP, head)

    @pl.when(core[0] != 0)
    def _():
        residue(late_field, lambda rows: measured[0, rows, :], jnp.where(live[0] > 0, 1.0, 0.0))

    real, imag = transform(chi[0], chi[1], far, True)

    @pl.when(core[0] == 0)
    def _():
        conj_times(patch, real, imag, half)
        conj_times(psi, real, imag, send)

    @pl.when(core[0] != 0)
    def _():
        conj_times(late_patch, real, imag, half)
        conj_times(psi, real, imag, stay)

    real, imag = transform(half[0].astype(jnp.float32), half[1].astype(jnp.float32), prop, True)

    @pl.when(core[0] == 0)
    def _():
        conj_times(rolled, real, imag, stay)

    @pl.when(core[0] != 0)
    def _():
        conj_times(rolled, real, imag, send)


def place_kernel(offsets, before, core, stay, came, out, staged, sems):
    row, col = offsets[0, 0], offsets[0, 1]
    row_before, col_before = before[0, 0], before[0, 1]

    def place(own, spill):
        copies = []
        for index, start in enumerate(range(0, W, FLUSH)):
            for inner in range(start, start + FLUSH, STEP):
                rows = pl.ds(inner, STEP)
                for part in range(2):
                    mine = jnp.where(inner + iota(0) >= row, own[part, rows, :].astype(jnp.float32), 0.0)
                    theirs = jnp.where(inner + iota(0) < row_before, spill[part, rows, :].astype(jnp.float32), 0.0)
                    here, there = iota(1) >= col, iota(1) >= col_before
                    staged[part, 0, rows, :W] = jnp.where(here, mine, 0.0) + jnp.where(there, theirs, 0.0)
                    staged[part, 0, rows, W:] = jnp.where(here, 0.0, mine) + jnp.where(there, 0.0, theirs)
            block = (slice(None), slice(None), pl.ds(start, FLUSH))
            copies.append(pltpu.make_async_copy(staged.at[block], out.at[block], sems.at[index]))
            copies[-1].start()
        for copy in copies:
            copy.wait()

    @pl.when(core[0] == 0)
    def _():
        place(came, stay)

    @pl.when(core[0] != 0)
    def _():
        place(stay, came)


def call(kernel, outs, specs, scratch=(), out_spec=VMEM, mib=16):
    return pl.pallas_call(
        kernel,
        out_shape=outs,
        in_specs=[{"s": SMEM, "v": VMEM, "a": ANY}[s] for s in specs],
        out_specs=jax.tree.map(lambda _: out_spec, outs),
        scratch_shapes=scratch,
        compiler_params=pltpu.CompilerParams(vmem_limit_bytes=mib << 20),
    )


def shaped(shape, dtype):
    return jax.ShapeDtypeStruct(shape, dtype)


WAVE = shaped((2, W, W), jnp.float32)
HALF_WAVE = shaped((2, W, W), jnp.bfloat16)
CODED = shaped((2, W + HEAD, W), jnp.int16)
CHI = pltpu.VMEM((2, W, W), jnp.float32)


def on_device(transmission, illumination, measured, offsets, live_count):
    prop, far = (jnp.asarray(t) for t in tables())
    count = lax.axis_size("tile")
    core = lax.axis_index("cuts").astype(jnp.int32)[None]

    def permute(value, target):
        pairs = []
        for c in range(2):
            for k in range(count):
                to_core, to_tile = target(c, k)
                pairs.append((c * count + k, to_core * count + to_tile % count))
        return lax.ppermute(value, ("cuts", "tile"), pairs)

    before = permute(offsets, lambda c, k: (c, k + 1))
    place = (offsets, before, core)
    encode = call(encode_kernel, CODED, "ssv")
    ahead = encode(offsets, live_count, transmission)
    direct = permute(ahead, lambda c, k: (0, k + 1) if c == 0 else (1, k - ASIDE))
    behind, mixed = call(mixed_kernel, (CODED, CODED), "sssvv")(before, core, live_count, transmission, measured)
    crossed = permute(ahead, lambda c, k: (1, k) if c == 0 else (0, k + 1))
    border = permute(mixed, lambda c, k: (0, k + 1) if c == 0 else (1, k - 1))
    edge = permute(behind, lambda c, k: (1, k - 1) if c == 0 else (0, k))
    rolled = call(roll_kernel, WAVE, "sssv")(*place, illumination)
    early = call(first_kernel, HALF_WAVE, "sssvvvv", [CHI])(*place, direct, transmission, rolled, prop)
    psi, patch, field = call(second_kernel, (HALF_WAVE, WAVE, WAVE), "sss" + "v" * 6, [CHI])(
        *place, crossed, edge, rolled, early, prop, far
    )
    late_patch, late_field = call(late_kernel, (WAVE, WAVE), "ssvvvv", [CHI])(
        offsets, core, border, transmission, psi, far
    )
    send, stay = call(
        third_kernel, (HALF_WAVE, HALF_WAVE), "ss" + "v" * 11, [CHI, pltpu.VMEM((2, W, W), jnp.bfloat16)]
    )(core, live_count, direct, border, measured, field, late_field, psi, patch, late_patch, rolled, prop, far)
    came = permute(send, lambda c, k: (1 - c, k))
    return call(
        place_kernel,
        shaped(transmission.shape, jnp.float32),
        "sssvv",
        [pltpu.VMEM(transmission.shape, jnp.float32), pltpu.SemaphoreType.DMA((W // FLUSH,))],
        ANY,
    )(*place, stay, came)


def solution(mesh):
    placed = (P(None, "cuts", "tile", None), P(), P("tile", None, None), P("tile", None), P("tile"))
    return jax.shard_map(
        on_device,
        mesh=mesh,
        in_specs=placed,
        out_specs=P(None, "cuts", "tile", None),
        check_vma=False,
    )
```

```python
import functools
import math

import jax
import jax.numpy as jnp
import numpy as np
from jax import lax
from jax.experimental import pallas as pl
from jax.experimental.pallas import tpu as pltpu
from jax.sharding import PartitionSpec as P


W = 256
H = W // 2
HEAD = 16
TOP = 32000.0
STEP = 32
ASIDE = 16
FLUSH = 64
LAST_PASSES = 1
MEASURED_STEP = 5.0 / TOP
VMEM = pl.BlockSpec(memory_space=pltpu.VMEM)
ANY = pl.BlockSpec(memory_space=pl.ANY)
SMEM = pl.BlockSpec(memory_space=pltpu.SMEM)


def split_table(matrix):
    parts = []
    for factor in (matrix.real, matrix.imag - matrix.real, matrix.real + matrix.imag):
        factor = np.asarray(factor, np.float32)
        high = factor.astype(jnp.bfloat16)
        low = (factor - high.astype(np.float32)).astype(jnp.bfloat16)
        parts += [high, low]
    return np.stack(parts)


def embedded(matrix):
    real = np.block([[matrix.real, -matrix.imag], [matrix.imag, matrix.real]]).astype(np.float32)
    parts = []
    for value in (real, real.T):
        high = value.astype(jnp.bfloat16)
        parts += [high, (value - high.astype(np.float32)).astype(jnp.bfloat16)]
    return parts


@functools.lru_cache(None)
def tables():
    freq = np.arange(W)
    signed = np.where(freq < W // 2, freq, freq - W).astype(np.float64)
    phase = np.pi * signed * signed / (4 * W)
    basis = np.exp(2j * np.pi * ((freq[:, None] * freq[None, :]) % W) / W)
    prop = (basis * np.exp(-1j * phase)[None, :]) @ np.conj(basis).T / W
    far = np.conj(basis) / math.sqrt(W)
    same, cross = prop[:H, :H], prop[:H, H:]
    return np.stack(embedded((same + cross) / 2) + embedded((same - cross) / 2)), split_table(far)


def halves(value):
    high = value.astype(jnp.bfloat16)
    low = (value - high.astype(jnp.float32)).astype(jnp.bfloat16)
    return high, low


def dot(first, second):
    return jnp.dot(first, second, preferred_element_type=jnp.float32)


def right(value, table, which):
    high, low = halves(value)
    big, small = table[2 * which], table[2 * which + 1]
    return dot(high, big) + dot(low, big) + dot(high, small)


def left(value, table, which):
    high, low = halves(value)
    big, small = table[2 * which], table[2 * which + 1]
    return dot(big, high) + dot(big, low) + dot(small, high)


def product(times, real, imag, table, conj):
    both = times(real + imag, table, 0)
    if conj:
        return both + times(imag, table, 1), both - times(real, table, 2)
    return both - times(imag, table, 2), both + times(real, table, 1)


def transform(real, imag, table, conj):
    real, imag = product(right, real, imag, table, conj)
    return product(left, real, imag, table, conj)


def set_parts(ops, which, rows, cols, value, passes):
    high = value.astype(jnp.bfloat16)
    ops[2 * which, rows, cols] = high
    if passes > 1:
        ops[2 * which + 1, rows, cols] = (value - high.astype(jnp.float32)).astype(jnp.bfloat16)


def circulant_dots(ops, prop, acc, side, passes):
    for which in range(2):
        high, low = ops[2 * which], ops[2 * which + 1]
        table = 4 * which + (2 if side == "right" else 0)
        big, small = prop[table], prop[table + 1]
        if side == "right":
            acc[which] = dot(high, big) + dot(low, big) + dot(high, small) if passes > 1 else dot(high, big)
        else:
            acc[which] = dot(big, high) + dot(big, low) + dot(small, high) if passes > 1 else dot(big, high)


def propagate(given, prop, ops, acc, passes, conj):
    sign = -1.0 if conj else 1.0
    left_half, right_half = pl.ds(0, H), pl.ds(H, H)
    for start in range(0, W, STEP):
        rows = pl.ds(start, STEP)
        real, imag = given(rows, start)
        for value, cols in ((real, left_half), (sign * imag if conj else imag, right_half)):
            set_parts(ops, 0, rows, cols, value[:, :H] + value[:, H:], passes)
            set_parts(ops, 1, rows, cols, value[:, :H] - value[:, H:], passes)
    circulant_dots(ops, prop, acc, "right", passes)
    for start in range(0, H, STEP):
        upper, lower = pl.ds(start, STEP), pl.ds(H + start, STEP)
        for source, target in ((left_half, upper), (right_half, lower)):
            plus_upper, minus_upper = acc[0, upper, source], acc[1, upper, source]
            plus_lower, minus_lower = acc[0, lower, source], acc[1, lower, source]
            for cols, top, bottom in (
                (left_half, plus_upper + minus_upper, plus_lower + minus_lower),
                (right_half, plus_upper - minus_upper, plus_lower - minus_lower),
            ):
                set_parts(ops, 0, target, cols, top + bottom, passes)
                set_parts(ops, 1, target, cols, top - bottom, passes)
    circulant_dots(ops, prop, acc, "left", passes)


def propagated(acc, start, conj):
    inner = start % H
    real, imag = (
        acc[0, pl.ds(row, STEP), :] + acc[1, pl.ds(row, STEP), :]
        if start < H
        else acc[0, pl.ds(row, STEP), :] - acc[1, pl.ds(row, STEP), :]
        for row in (inner, H + inner)
    )
    return real, -imag if conj else imag


def iota(dim):
    return lax.broadcasted_iota(jnp.int32, (STEP, W), dim)


def windowed(full, part, rows, col):
    return jnp.where(iota(1) >= col, full[part, rows, :W], full[part, rows, W:])


def at_core():
    return lax.axis_index("cuts")


def spread(offsets, which):
    return jnp.broadcast_to(offsets[0:1, which : which + 1], (STEP, W))


def encode_kernel(offsets, live, own, coded):
    col = spread(offsets, 1)
    held = own.at[:, 0]
    peak = jnp.zeros((8, W), jnp.float32)
    for start in range(0, W, STEP):
        rows = pl.ds(start, STEP)
        real, imag = windowed(held, 0, rows, col), windowed(held, 1, rows, col)
        high = jnp.maximum(jnp.abs(real), jnp.abs(imag))
        for piece in range(0, STEP, 8):
            peak = jnp.maximum(peak, high[piece : piece + 8])
    peak = jnp.max(jnp.max(peak, axis=1, keepdims=True), axis=0, keepdims=True)
    peak = jnp.broadcast_to(jnp.maximum(peak, 1e-30), (1, W))
    power = jnp.ceil(jnp.log(peak) * (1.0 / math.log(2.0)))
    gain = jnp.exp2(-power) * TOP
    for part in range(2):
        for start in range(0, W, STEP):
            rows = pl.ds(start, STEP)
            scaled = jnp.round(windowed(held, part, rows, col) * gain)
            coded[part, rows, :] = scaled.astype(jnp.int32).astype(jnp.int16)
    flag = jnp.where(live[0] > 0, 1, 0)
    coded[0, pl.ds(W, HEAD), :] = jnp.broadcast_to(power.astype(jnp.int32), (HEAD, W)).astype(jnp.int16)
    coded[1, pl.ds(W, HEAD), :] = jnp.full((HEAD, W), flag, jnp.int32).astype(jnp.int16)


def mixed_kernel(before, live, own, measured, coded, mixed):
    encode_kernel(before, live, own, coded)

    @pl.when(at_core() == 0)
    def _():
        for start in range(0, W, STEP):
            rows = pl.ds(start, STEP)
            scaled = jnp.round(measured[0, rows, :] * (1.0 / MEASURED_STEP))
            mixed[0, rows, :] = scaled.astype(jnp.int32).astype(jnp.int16)

    @pl.when(at_core() != 0)
    def _():
        mixed[...] = coded[...]


def head_of(coded, part):
    return coded[part, pl.ds(W, HEAD), :].astype(jnp.int32).astype(jnp.float32)[0:1]


def gain_of(coded):
    return jnp.exp2(head_of(coded, 0)) * (1.0 / TOP)


def decoded(coded, part, rows, gain):
    return coded[part, rows, :].astype(jnp.int32).astype(jnp.float32) * gain


def roll_kernel(offsets, before, illumination, rolled):
    row = lax.rem(jnp.where(at_core() == 0, before[0, 0], offsets[0, 0]), W)
    col = lax.rem(jnp.where(at_core() == 0, before[0, 1], offsets[0, 1]), W)
    for part in range(2):
        rolled[part] = pltpu.roll(pltpu.roll(illumination[part], row, 0), col, 1)


def multiplied(wave, patch):
    def rows_of(rows, start):
        wave_real, wave_imag = wave[0, rows, :].astype(jnp.float32), wave[1, rows, :].astype(jnp.float32)
        patch_real, patch_imag = patch(0, rows, start), patch(1, rows, start)
        return wave_real * patch_real - wave_imag * patch_imag, wave_real * patch_imag + wave_imag * patch_real

    return rows_of


def times_patch(wave, patch, out):
    product_of = multiplied(wave, patch)
    for start in range(0, W, STEP):
        rows = pl.ds(start, STEP)
        out[0, rows, :], out[1, rows, :] = product_of(rows, start)


def chosen(row, upper, lower):
    return lambda part, rows, start: jnp.where(
        start + iota(0) >= row, lower(part, rows), upper(part, rows)
    )


def first_slice(rolled, patch, prop, psi, ops, acc):
    propagate(multiplied(rolled, patch), prop, ops, acc, 3, False)
    for start in range(0, W, STEP):
        rows = pl.ds(start, STEP)
        real, imag = propagated(acc, start, False)
        psi[0, rows, :] = real.astype(jnp.bfloat16)
        psi[1, rows, :] = imag.astype(jnp.bfloat16)


def first_kernel(offsets, before, direct, own, rolled, prop, psi, ops, acc):
    @pl.when(at_core() == 0)
    def _():
        gain = gain_of(direct)
        local = own.at[:, 0]
        col = spread(before, 1)
        patch = chosen(
            spread(before, 0),
            lambda part, rows: windowed(local, part, rows, col),
            lambda part, rows: decoded(direct, part, rows, gain),
        )
        first_slice(rolled, patch, prop, psi, ops, acc)


def keeping(given, patch):
    def kept(part, rows, start):
        value = given(part, rows, start)
        patch[part, rows, :] = value
        return value

    return kept


def second_slice(given, psi, far, patch, field, chi):
    times_patch(psi, keeping(given, patch), chi)
    out_real, out_imag = transform(chi[0], chi[1], far, False)
    field[0] = out_real
    field[1] = out_imag


def second_kernel(offsets, before, crossed, edge, rolled, early, prop, far, psi, patch, field, chi, ops, acc):
    row = jnp.where(at_core() == 0, spread(before, 0), spread(offsets, 0))
    gain_crossed, gain_edge = gain_of(crossed), gain_of(edge)
    given = chosen(
        row,
        lambda part, rows: decoded(edge, part, rows, gain_edge),
        lambda part, rows: decoded(crossed, part, rows, gain_crossed),
    )

    @pl.when(at_core() == 0)
    def _():
        psi[...] = early[...]
        second_slice(given, psi, far, patch, field, chi)

    @pl.when(at_core() != 0)
    def _():
        first_slice(rolled, given, prop, psi, ops, acc)


def conj_times(first, real, imag, out):
    for start in range(0, W, STEP):
        rows = pl.ds(start, STEP)
        keep = slice(start, start + STEP)
        first_real, first_imag = first[0, rows, :].astype(jnp.float32), first[1, rows, :].astype(jnp.float32)
        out[0, rows, :] = (first_real * real[keep] + first_imag * imag[keep]).astype(out.dtype)
        out[1, rows, :] = (first_real * imag[keep] - first_imag * real[keep]).astype(out.dtype)


def third_kernel(
    offsets, live, direct, border, own, measured, field, psi, patch, rolled, prop, far, send, stay,
    chi, half, late_patch, late_field, ops, acc,
):
    @pl.when(at_core() != 0)
    def _():
        gain_border = gain_of(border)
        local = own.at[:, 0]
        col = spread(offsets, 1)
        last = chosen(
            spread(offsets, 0),
            lambda part, rows: decoded(border, part, rows, gain_border),
            lambda part, rows: windowed(local, part, rows, col),
        )
        second_slice(last, psi, far, late_patch, late_field, chi)

    def residue(field, target, alive):
        for start in range(0, W, STEP):
            rows = pl.ds(start, STEP)
            real, imag = field[0, rows, :], field[1, rows, :]
            weight = (real * real + imag * imag - target(rows)) * alive
            chi[0, rows, :] = weight * real
            chi[1, rows, :] = weight * imag

    @pl.when(at_core() == 0)
    def _():
        head = head_of(direct, 1)
        residue(field, lambda rows: border[0, rows, :].astype(jnp.int32).astype(jnp.float32) * MEASURED_STEP, head)

    @pl.when(at_core() != 0)
    def _():
        residue(late_field, lambda rows: measured[0, rows, :], jnp.where(live[0] > 0, 1.0, 0.0))

    real, imag = transform(chi[0], chi[1], far, True)

    @pl.when(at_core() == 0)
    def _():
        conj_times(patch, real, imag, half)
        conj_times(psi, real, imag, send)

    @pl.when(at_core() != 0)
    def _():
        conj_times(late_patch, real, imag, half)
        conj_times(psi, real, imag, stay)

    propagate(
        lambda rows, start: (half[0, rows, :].astype(jnp.float32), half[1, rows, :].astype(jnp.float32)),
        prop,
        ops,
        acc,
        LAST_PASSES,
        True,
    )

    def last(out):
        for start in range(0, W, STEP):
            rows = pl.ds(start, STEP)
            real, imag = propagated(acc, start, True)
            wave_real, wave_imag = rolled[0, rows, :], rolled[1, rows, :]
            out[0, rows, :] = (wave_real * real + wave_imag * imag).astype(out.dtype)
            out[1, rows, :] = (wave_real * imag - wave_imag * real).astype(out.dtype)

    @pl.when(at_core() == 0)
    def _():
        last(stay)

    @pl.when(at_core() != 0)
    def _():
        last(send)


def place_kernel(offsets, before, stay, came, out, staged, sems):
    row, col = spread(offsets, 0), spread(offsets, 1)
    row_before, col_before = spread(before, 0), spread(before, 1)

    def place(own, spill):
        copies = []
        for index, start in enumerate(range(0, W, FLUSH)):
            for inner in range(start, start + FLUSH, STEP):
                rows = pl.ds(inner, STEP)
                for part in range(2):
                    mine = jnp.where(inner + iota(0) >= row, own[part, rows, :].astype(jnp.float32), 0.0)
                    theirs = jnp.where(inner + iota(0) < row_before, spill[part, rows, :].astype(jnp.float32), 0.0)
                    here, there = iota(1) >= col, iota(1) >= col_before
                    staged[part, 0, rows, :W] = jnp.where(here, mine, 0.0) + jnp.where(there, theirs, 0.0)
                    staged[part, 0, rows, W:] = jnp.where(here, 0.0, mine) + jnp.where(there, 0.0, theirs)
            block = (slice(None), slice(None), pl.ds(start, FLUSH))
            copies.append(pltpu.make_async_copy(staged.at[block], out.at[block], sems.at[index]))
            copies[-1].start()
        for copy in copies:
            copy.wait()

    @pl.when(at_core() == 0)
    def _():
        place(came, stay)

    @pl.when(at_core() != 0)
    def _():
        place(stay, came)


def call(kernel, outs, specs, scratch=(), out_spec=VMEM, mib=16):
    return pl.pallas_call(
        kernel,
        out_shape=outs,
        in_specs=[{"s": SMEM, "v": VMEM, "a": ANY}[s] for s in specs],
        out_specs=jax.tree.map(lambda _: out_spec, outs),
        scratch_shapes=scratch,
        compiler_params=pltpu.CompilerParams(vmem_limit_bytes=mib << 20),
    )


def shaped(shape, dtype):
    return jax.ShapeDtypeStruct(shape, dtype)


WAVE = shaped((2, W, W), jnp.float32)
HALF_WAVE = shaped((2, W, W), jnp.bfloat16)
CODED = shaped((2, W + HEAD, W), jnp.int16)
CHI = pltpu.VMEM((2, W, W), jnp.float32)
PROPAGATE = [pltpu.VMEM((4, W, W), jnp.bfloat16), pltpu.VMEM((2, W, W), jnp.float32)]


def on_device(transmission, illumination, measured, offsets, live_count):
    prop, far = (jnp.asarray(t) for t in tables())
    count = lax.axis_size("tile")

    def permute(value, target):
        pairs = []
        for c in range(2):
            for k in range(count):
                to_core, to_tile = target(c, k)
                pairs.append((c * count + k, to_core * count + to_tile % count))
        return lax.ppermute(value, ("cuts", "tile"), pairs)

    before = permute(offsets, lambda c, k: (c, k + 1))
    place = (offsets, before)
    encode = call(encode_kernel, CODED, "vsv")
    ahead = encode(offsets, live_count, transmission)
    direct = permute(ahead, lambda c, k: (0, k + 1) if c == 0 else (1, k - ASIDE))
    behind, mixed = call(mixed_kernel, (CODED, CODED), "vsvv")(
        before, live_count, transmission, measured
    )
    crossed = permute(ahead, lambda c, k: (1, k) if c == 0 else (0, k + 1))
    border = permute(mixed, lambda c, k: (0, k + 1) if c == 0 else (1, k - 1))
    edge = permute(behind, lambda c, k: (1, k - 1) if c == 0 else (0, k))
    rolled = call(roll_kernel, WAVE, "ssv")(*place, illumination)
    early = call(first_kernel, HALF_WAVE, "vvvvvv", PROPAGATE)(*place, direct, transmission, rolled, prop)
    psi, patch, field = call(second_kernel, (HALF_WAVE, WAVE, WAVE), "v" * 8, [CHI, *PROPAGATE])(
        *place, crossed, edge, rolled, early, prop, far
    )
    send, stay = call(
        third_kernel,
        (HALF_WAVE, HALF_WAVE),
        "vs" + "v" * 10,
        [CHI, pltpu.VMEM((2, W, W), jnp.bfloat16), CHI, CHI, *PROPAGATE],
    )(offsets, live_count, direct, border, transmission, measured, field, psi, patch, rolled, prop, far)
    came = permute(send, lambda c, k: (1 - c, k))
    return call(
        place_kernel,
        shaped(transmission.shape, jnp.float32),
        "vvvv",
        [pltpu.VMEM(transmission.shape, jnp.float32), pltpu.SemaphoreType.DMA((W // FLUSH,))],
        ANY,
    )(*place, stay, came)


def solution(mesh):
    placed = (P(None, "cuts", "tile", None), P(), P("tile", None, None), P("tile", None), P("tile"))
    return jax.shard_map(
        on_device,
        mesh=mesh,
        in_specs=placed,
        out_specs=P(None, "cuts", "tile", None),
        check_vma=False,
    )
```

```python
import functools
import math

import jax
import jax.numpy as jnp
import numpy as np
from jax import lax
from jax.experimental import pallas as pl
from jax.experimental.pallas import tpu as pltpu
from jax.sharding import PartitionSpec as P


W = 256
H = W // 2
HEAD = 16
TOP = 32000.0
STEP = 32
ASIDE = 16
FLUSH = 64
LAST_PASSES = 1
MEASURED_STEP = 5.0 / TOP
VMEM = pl.BlockSpec(memory_space=pltpu.VMEM)
ANY = pl.BlockSpec(memory_space=pl.ANY)
SMEM = pl.BlockSpec(memory_space=pltpu.SMEM)


def split_table(matrix):
    parts = []
    for factor in (matrix.real, matrix.imag - matrix.real, matrix.real + matrix.imag):
        factor = np.asarray(factor, np.float32)
        high = factor.astype(jnp.bfloat16)
        low = (factor - high.astype(np.float32)).astype(jnp.bfloat16)
        parts += [high, low]
    return np.stack(parts)


def embedded(matrix):
    real = np.block([[matrix.real, -matrix.imag], [matrix.imag, matrix.real]]).astype(np.float32)
    parts = []
    for value in (real, real.T):
        high = value.astype(jnp.bfloat16)
        parts += [high, (value - high.astype(np.float32)).astype(jnp.bfloat16)]
    return parts


@functools.lru_cache(None)
def tables():
    freq = np.arange(W)
    signed = np.where(freq < W // 2, freq, freq - W).astype(np.float64)
    phase = np.pi * signed * signed / (4 * W)
    basis = np.exp(2j * np.pi * ((freq[:, None] * freq[None, :]) % W) / W)
    prop = (basis * np.exp(-1j * phase)[None, :]) @ np.conj(basis).T / W
    far = np.conj(basis) / math.sqrt(W)
    same, cross = prop[:H, :H], prop[:H, H:]
    return np.stack(embedded((same + cross) / 2) + embedded((same - cross) / 2)), split_table(far)


def halves(value):
    high = value.astype(jnp.bfloat16)
    low = (value - high.astype(jnp.float32)).astype(jnp.bfloat16)
    return high, low


def dot(first, second):
    return jnp.dot(first, second, preferred_element_type=jnp.float32)


def right(value, table, which):
    high, low = halves(value)
    big, small = table[2 * which], table[2 * which + 1]
    return dot(high, big) + dot(low, big) + dot(high, small)


def left(value, table, which):
    high, low = halves(value)
    big, small = table[2 * which], table[2 * which + 1]
    return dot(big, high) + dot(big, low) + dot(small, high)


def product(times, real, imag, table, conj):
    both = times(real + imag, table, 0)
    if conj:
        return both + times(imag, table, 1), both - times(real, table, 2)
    return both - times(imag, table, 2), both + times(real, table, 1)


def transform(real, imag, table, conj):
    real, imag = product(right, real, imag, table, conj)
    return product(left, real, imag, table, conj)


def set_parts(ops, which, rows, cols, value, passes):
    high = value.astype(jnp.bfloat16)
    ops[2 * which, rows, cols] = high
    if passes > 1:
        ops[2 * which + 1, rows, cols] = (value - high.astype(jnp.float32)).astype(jnp.bfloat16)


def circulant_dots(ops, prop, acc, side, passes):
    for which in range(2):
        high, low = ops[2 * which], ops[2 * which + 1]
        table = 4 * which + (2 if side == "right" else 0)
        big, small = prop[table], prop[table + 1]
        if side == "right":
            acc[which] = dot(high, big) + dot(low, big) + dot(high, small) if passes > 1 else dot(high, big)
        else:
            acc[which] = dot(big, high) + dot(big, low) + dot(small, high) if passes > 1 else dot(big, high)


def propagate(given, prop, ops, acc, passes, conj):
    sign = -1.0 if conj else 1.0
    left_half, right_half = pl.ds(0, H), pl.ds(H, H)
    for start in range(0, W, STEP):
        rows = pl.ds(start, STEP)
        real, imag = given(rows, start)
        for value, cols in ((real, left_half), (sign * imag if conj else imag, right_half)):
            set_parts(ops, 0, rows, cols, value[:, :H] + value[:, H:], passes)
            set_parts(ops, 1, rows, cols, value[:, :H] - value[:, H:], passes)
    circulant_dots(ops, prop, acc, "right", passes)
    for start in range(0, H, STEP):
        upper, lower = pl.ds(start, STEP), pl.ds(H + start, STEP)
        for source, target in ((left_half, upper), (right_half, lower)):
            plus_upper, minus_upper = acc[0, upper, source], acc[1, upper, source]
            plus_lower, minus_lower = acc[0, lower, source], acc[1, lower, source]
            for cols, top, bottom in (
                (left_half, plus_upper + minus_upper, plus_lower + minus_lower),
                (right_half, plus_upper - minus_upper, plus_lower - minus_lower),
            ):
                set_parts(ops, 0, target, cols, top + bottom, passes)
                set_parts(ops, 1, target, cols, top - bottom, passes)
    circulant_dots(ops, prop, acc, "left", passes)


def propagated(acc, start, conj):
    inner = start % H
    real, imag = (
        acc[0, pl.ds(row, STEP), :] + acc[1, pl.ds(row, STEP), :]
        if start < H
        else acc[0, pl.ds(row, STEP), :] - acc[1, pl.ds(row, STEP), :]
        for row in (inner, H + inner)
    )
    return real, -imag if conj else imag


def iota(dim):
    return lax.broadcasted_iota(jnp.int32, (STEP, W), dim)


def windowed(full, part, rows, col):
    return jnp.where(iota(1) >= col, full[part, rows, :W], full[part, rows, W:])


def at_core():
    return lax.axis_index("cuts")


def spread(offsets, which):
    return jnp.broadcast_to(offsets[0:1, which : which + 1], (STEP, W))


def encode_kernel(offsets, live, own, coded):
    col = spread(offsets, 1)
    held = own.at[:, 0]
    peak = jnp.zeros((8, W), jnp.float32)
    for start in range(0, W, STEP):
        rows = pl.ds(start, STEP)
        real, imag = windowed(held, 0, rows, col), windowed(held, 1, rows, col)
        high = jnp.maximum(jnp.abs(real), jnp.abs(imag))
        for piece in range(0, STEP, 8):
            peak = jnp.maximum(peak, high[piece : piece + 8])
    peak = jnp.max(jnp.max(peak, axis=1, keepdims=True), axis=0, keepdims=True)
    peak = jnp.broadcast_to(jnp.maximum(peak, 1e-30), (1, W))
    power = jnp.ceil(jnp.log(peak) * (1.0 / math.log(2.0)))
    gain = jnp.exp2(-power) * TOP
    for part in range(2):
        for start in range(0, W, STEP):
            rows = pl.ds(start, STEP)
            scaled = jnp.round(windowed(held, part, rows, col) * gain)
            coded[part, rows, :] = scaled.astype(jnp.int32).astype(jnp.int16)
    flag = jnp.where(live[0] > 0, 1, 0)
    coded[0, pl.ds(W, HEAD), :] = jnp.broadcast_to(power.astype(jnp.int32), (HEAD, W)).astype(jnp.int16)
    coded[1, pl.ds(W, HEAD), :] = jnp.full((HEAD, W), flag, jnp.int32).astype(jnp.int16)


def mixed_kernel(before, live, own, measured, coded, mixed):
    encode_kernel(before, live, own, coded)

    @pl.when(at_core() == 0)
    def _():
        for start in range(0, W, STEP):
            rows = pl.ds(start, STEP)
            scaled = jnp.round(measured[0, rows, :] * (1.0 / MEASURED_STEP))
            mixed[0, rows, :] = scaled.astype(jnp.int32).astype(jnp.int16)

    @pl.when(at_core() != 0)
    def _():
        mixed[...] = coded[...]


def head_of(coded, part):
    return coded[part, pl.ds(W, HEAD), :].astype(jnp.int32).astype(jnp.float32)[0:1]


def gain_of(coded):
    return jnp.exp2(head_of(coded, 0)) * (1.0 / TOP)


def decoded(coded, part, rows, gain):
    return coded[part, rows, :].astype(jnp.int32).astype(jnp.float32) * gain


def roll_kernel(offsets, before, illumination, rolled):
    row = lax.rem(jnp.where(at_core() == 0, before[0, 0], offsets[0, 0]), W)
    col = lax.rem(jnp.where(at_core() == 0, before[0, 1], offsets[0, 1]), W)
    for part in range(2):
        rolled[part] = pltpu.roll(pltpu.roll(illumination[part], row, 0), col, 1)


def multiplied(wave, patch):
    def rows_of(rows, start):
        wave_real, wave_imag = wave[0, rows, :].astype(jnp.float32), wave[1, rows, :].astype(jnp.float32)
        patch_real, patch_imag = patch(0, rows, start), patch(1, rows, start)
        return wave_real * patch_real - wave_imag * patch_imag, wave_real * patch_imag + wave_imag * patch_real

    return rows_of


def times_patch(wave, patch, out):
    product_of = multiplied(wave, patch)
    for start in range(0, W, STEP):
        rows = pl.ds(start, STEP)
        out[0, rows, :], out[1, rows, :] = product_of(rows, start)


def chosen(row, upper, lower):
    return lambda part, rows, start: jnp.where(
        start + iota(0) >= row, lower(part, rows), upper(part, rows)
    )


def first_slice(rolled, patch, prop, psi, ops, acc):
    propagate(multiplied(rolled, patch), prop, ops, acc, 3, False)
    for start in range(0, W, STEP):
        rows = pl.ds(start, STEP)
        real, imag = propagated(acc, start, False)
        psi[0, rows, :] = real.astype(jnp.bfloat16)
        psi[1, rows, :] = imag.astype(jnp.bfloat16)


def first_kernel(offsets, before, direct, own, rolled, prop, psi, ops, acc):
    @pl.when(at_core() == 0)
    def _():
        gain = gain_of(direct)
        local = own.at[:, 0]
        col = spread(before, 1)
        patch = chosen(
            spread(before, 0),
            lambda part, rows: windowed(local, part, rows, col),
            lambda part, rows: decoded(direct, part, rows, gain),
        )
        first_slice(rolled, patch, prop, psi, ops, acc)


def keeping(given, patch):
    def kept(part, rows, start):
        value = given(part, rows, start)
        patch[part, rows, :] = value
        return value

    return kept


def second_slice(given, psi, far, patch, field, chi):
    times_patch(psi, keeping(given, patch), chi)
    out_real, out_imag = transform(chi[0], chi[1], far, False)
    field[0] = out_real
    field[1] = out_imag


def second_kernel(offsets, before, crossed, edge, rolled, early, prop, far, psi, patch, field, chi, ops, acc):
    row = jnp.where(at_core() == 0, spread(before, 0), spread(offsets, 0))
    gain_crossed, gain_edge = gain_of(crossed), gain_of(edge)
    given = chosen(
        row,
        lambda part, rows: decoded(edge, part, rows, gain_edge),
        lambda part, rows: decoded(crossed, part, rows, gain_crossed),
    )

    @pl.when(at_core() == 0)
    def _():
        psi[...] = early[...]
        second_slice(given, psi, far, patch, field, chi)

    @pl.when(at_core() != 0)
    def _():
        first_slice(rolled, given, prop, psi, ops, acc)


def conj_times(first, real, imag, out):
    for start in range(0, W, STEP):
        rows = pl.ds(start, STEP)
        keep = slice(start, start + STEP)
        first_real, first_imag = first[0, rows, :].astype(jnp.float32), first[1, rows, :].astype(jnp.float32)
        out[0, rows, :] = (first_real * real[keep] + first_imag * imag[keep]).astype(out.dtype)
        out[1, rows, :] = (first_real * imag[keep] - first_imag * real[keep]).astype(out.dtype)


def last_slice(half, rolled, prop, out, ops, acc):
    propagate(
        lambda rows, start: (half[0, rows, :].astype(jnp.float32), half[1, rows, :].astype(jnp.float32)),
        prop,
        ops,
        acc,
        LAST_PASSES,
        True,
    )
    for start in range(0, W, STEP):
        rows = pl.ds(start, STEP)
        real, imag = propagated(acc, start, True)
        wave_real, wave_imag = rolled[0, rows, :], rolled[1, rows, :]
        out[0, rows, :] = (wave_real * real + wave_imag * imag).astype(out.dtype)
        out[1, rows, :] = (wave_real * imag - wave_imag * real).astype(out.dtype)


def third_kernel(
    offsets, live, direct, border, own, measured, field, psi, patch, rolled, prop, far, send, early, half,
    chi, late_patch, late_field, ops, acc,
):
    @pl.when(at_core() != 0)
    def _():
        gain_border = gain_of(border)
        local = own.at[:, 0]
        col = spread(offsets, 1)
        last = chosen(
            spread(offsets, 0),
            lambda part, rows: decoded(border, part, rows, gain_border),
            lambda part, rows: windowed(local, part, rows, col),
        )
        second_slice(last, psi, far, late_patch, late_field, chi)

    def residue(field, target, alive):
        for start in range(0, W, STEP):
            rows = pl.ds(start, STEP)
            real, imag = field[0, rows, :], field[1, rows, :]
            weight = (real * real + imag * imag - target(rows)) * alive
            chi[0, rows, :] = weight * real
            chi[1, rows, :] = weight * imag

    @pl.when(at_core() == 0)
    def _():
        head = head_of(direct, 1)
        residue(field, lambda rows: border[0, rows, :].astype(jnp.int32).astype(jnp.float32) * MEASURED_STEP, head)

    @pl.when(at_core() != 0)
    def _():
        residue(late_field, lambda rows: measured[0, rows, :], jnp.where(live[0] > 0, 1.0, 0.0))

    real, imag = transform(chi[0], chi[1], far, True)

    @pl.when(at_core() == 0)
    def _():
        conj_times(patch, real, imag, half)
        conj_times(psi, real, imag, send)

    @pl.when(at_core() != 0)
    def _():
        conj_times(late_patch, real, imag, half)
        conj_times(psi, real, imag, early)
        last_slice(half, rolled, prop, send, ops, acc)


def fourth_kernel(half, rolled, early, prop, stay, ops, acc):
    @pl.when(at_core() == 0)
    def _():
        last_slice(half, rolled, prop, stay, ops, acc)

    @pl.when(at_core() != 0)
    def _():
        stay[...] = early[...]


def place_kernel(offsets, before, stay, came, out, staged, sems):
    row, col = spread(offsets, 0), spread(offsets, 1)
    row_before, col_before = spread(before, 0), spread(before, 1)

    def place(own, spill):
        copies = []
        for index, start in enumerate(range(0, W, FLUSH)):
            for inner in range(start, start + FLUSH, STEP):
                rows = pl.ds(inner, STEP)
                for part in range(2):
                    mine = jnp.where(inner + iota(0) >= row, own[part, rows, :].astype(jnp.float32), 0.0)
                    theirs = jnp.where(inner + iota(0) < row_before, spill[part, rows, :].astype(jnp.float32), 0.0)
                    here, there = iota(1) >= col, iota(1) >= col_before
                    staged[part, 0, rows, :W] = jnp.where(here, mine, 0.0) + jnp.where(there, theirs, 0.0)
                    staged[part, 0, rows, W:] = jnp.where(here, 0.0, mine) + jnp.where(there, 0.0, theirs)
            block = (slice(None), slice(None), pl.ds(start, FLUSH))
            copies.append(pltpu.make_async_copy(staged.at[block], out.at[block], sems.at[index]))
            copies[-1].start()
        for copy in copies:
            copy.wait()

    @pl.when(at_core() == 0)
    def _():
        place(came, stay)

    @pl.when(at_core() != 0)
    def _():
        place(stay, came)


def call(kernel, outs, specs, scratch=(), out_spec=VMEM, mib=16):
    return pl.pallas_call(
        kernel,
        out_shape=outs,
        in_specs=[{"s": SMEM, "v": VMEM, "a": ANY}[s] for s in specs],
        out_specs=jax.tree.map(lambda _: out_spec, outs),
        scratch_shapes=scratch,
        compiler_params=pltpu.CompilerParams(vmem_limit_bytes=mib << 20),
    )


def shaped(shape, dtype):
    return jax.ShapeDtypeStruct(shape, dtype)


WAVE = shaped((2, W, W), jnp.float32)
HALF_WAVE = shaped((2, W, W), jnp.bfloat16)
CODED = shaped((2, W + HEAD, W), jnp.int16)
CHI = pltpu.VMEM((2, W, W), jnp.float32)
PROPAGATE = [pltpu.VMEM((4, W, W), jnp.bfloat16), pltpu.VMEM((2, W, W), jnp.float32)]


def on_device(transmission, illumination, measured, offsets, live_count):
    prop, far = (jnp.asarray(t) for t in tables())
    count = lax.axis_size("tile")

    def permute(value, target):
        pairs = []
        for c in range(2):
            for k in range(count):
                to_core, to_tile = target(c, k)
                pairs.append((c * count + k, to_core * count + to_tile % count))
        return lax.ppermute(value, ("cuts", "tile"), pairs)

    before = permute(offsets, lambda c, k: (c, k + 1))
    place = (offsets, before)
    encode = call(encode_kernel, CODED, "vsv")
    ahead = encode(offsets, live_count, transmission)
    direct = permute(ahead, lambda c, k: (0, k + 1) if c == 0 else (1, k - ASIDE))
    behind, mixed = call(mixed_kernel, (CODED, CODED), "vsvv")(
        before, live_count, transmission, measured
    )
    crossed = permute(ahead, lambda c, k: (1, k) if c == 0 else (0, k + 1))
    border = permute(mixed, lambda c, k: (0, k + 1) if c == 0 else (1, k - 1))
    edge = permute(behind, lambda c, k: (1, k - 1) if c == 0 else (0, k))
    rolled = call(roll_kernel, WAVE, "ssv")(*place, illumination)
    early = call(first_kernel, HALF_WAVE, "vvvvvv", PROPAGATE)(*place, direct, transmission, rolled, prop)
    psi, patch, field = call(second_kernel, (HALF_WAVE, WAVE, WAVE), "v" * 8, [CHI, *PROPAGATE])(
        *place, crossed, edge, rolled, early, prop, far
    )
    send, early_stay, half = call(
        third_kernel, (HALF_WAVE, HALF_WAVE, HALF_WAVE), "vs" + "v" * 10, [CHI, CHI, CHI, *PROPAGATE]
    )(offsets, live_count, direct, border, transmission, measured, field, psi, patch, rolled, prop, far)
    came = permute(send, lambda c, k: (1 - c, k))
    stay = call(fourth_kernel, HALF_WAVE, "vvvv", PROPAGATE)(half, rolled, early_stay, prop)
    return call(
        place_kernel,
        shaped(transmission.shape, jnp.float32),
        "vvvv",
        [pltpu.VMEM(transmission.shape, jnp.float32), pltpu.SemaphoreType.DMA((W // FLUSH,))],
        ANY,
    )(*place, stay, came)


def solution(mesh):
    placed = (P(None, "cuts", "tile", None), P(), P("tile", None, None), P("tile", None), P("tile"))
    return jax.shard_map(
        on_device,
        mesh=mesh,
        in_specs=placed,
        out_specs=P(None, "cuts", "tile", None),
        check_vma=False,
    )
```

```python
import functools
import math

import jax
import jax.numpy as jnp
import numpy as np
from jax import lax
from jax.experimental import pallas as pl
from jax.experimental.pallas import tpu as pltpu
from jax.sharding import PartitionSpec as P


W = 256
H = W // 2
HEAD = 16
TOP = 32000.0
STEP = 16
ASIDE = 1
FLUSH = 32
LAST_PASSES = 1
MEASURED_STEP = 5.0 / TOP
VMEM = pl.BlockSpec(memory_space=pltpu.VMEM)
ANY = pl.BlockSpec(memory_space=pl.ANY)
SMEM = pl.BlockSpec(memory_space=pltpu.SMEM)


def split_table(matrix):
    parts = []
    for factor in (matrix.real, matrix.imag - matrix.real, matrix.real + matrix.imag):
        factor = np.asarray(factor, np.float32)
        high = factor.astype(jnp.bfloat16)
        low = (factor - high.astype(np.float32)).astype(jnp.bfloat16)
        parts += [high, low]
    return np.stack(parts)


def embedded(matrix):
    real = np.block([[matrix.real, -matrix.imag], [matrix.imag, matrix.real]]).astype(np.float32)
    parts = []
    for value in (real, real.T):
        high = value.astype(jnp.bfloat16)
        parts += [high, (value - high.astype(np.float32)).astype(jnp.bfloat16)]
    return parts


@functools.lru_cache(None)
def tables():
    freq = np.arange(W)
    signed = np.where(freq < W // 2, freq, freq - W).astype(np.float64)
    phase = np.pi * signed * signed / (4 * W)
    basis = np.exp(2j * np.pi * ((freq[:, None] * freq[None, :]) % W) / W)
    prop = (basis * np.exp(-1j * phase)[None, :]) @ np.conj(basis).T / W
    far = np.conj(basis) / math.sqrt(W)
    same, cross = prop[:H, :H], prop[:H, H:]
    return np.stack(embedded((same + cross) / 2) + embedded((same - cross) / 2)), split_table(far)


def halves(value):
    high = value.astype(jnp.bfloat16)
    low = (value - high.astype(jnp.float32)).astype(jnp.bfloat16)
    return high, low


def dot(first, second):
    return jnp.dot(first, second, preferred_element_type=jnp.float32)


def right(value, table, which):
    high, low = halves(value)
    big, small = table[2 * which], table[2 * which + 1]
    return dot(high, big) + dot(low, big) + dot(high, small)


def left(value, table, which):
    high, low = halves(value)
    big, small = table[2 * which], table[2 * which + 1]
    return dot(big, high) + dot(big, low) + dot(small, high)


def product(times, real, imag, table, conj):
    both = times(real + imag, table, 0)
    if conj:
        return both + times(imag, table, 1), both - times(real, table, 2)
    return both - times(imag, table, 2), both + times(real, table, 1)


def transform(real, imag, table, conj):
    real, imag = product(right, real, imag, table, conj)
    return product(left, real, imag, table, conj)


def set_parts(ops, which, rows, cols, value, passes):
    high = value.astype(jnp.bfloat16)
    ops[2 * which, rows, cols] = high
    if passes > 1:
        ops[2 * which + 1, rows, cols] = (value - high.astype(jnp.float32)).astype(jnp.bfloat16)


def circulant_dots(ops, prop, acc, side, passes):
    for which in range(2):
        high, low = ops[2 * which], ops[2 * which + 1]
        table = 4 * which + (2 if side == "right" else 0)
        big, small = prop[table], prop[table + 1]
        if side == "right":
            acc[which] = dot(high, big) + dot(low, big) + dot(high, small) if passes > 1 else dot(high, big)
        else:
            acc[which] = dot(big, high) + dot(big, low) + dot(small, high) if passes > 1 else dot(big, high)


def propagate(given, prop, ops, acc, passes, conj):
    sign = -1.0 if conj else 1.0
    left_half, right_half = pl.ds(0, H), pl.ds(H, H)
    for start in range(0, W, STEP):
        rows = pl.ds(start, STEP)
        real, imag = given(rows, start)
        for value, cols in ((real, left_half), (sign * imag if conj else imag, right_half)):
            set_parts(ops, 0, rows, cols, value[:, :H] + value[:, H:], passes)
            set_parts(ops, 1, rows, cols, value[:, :H] - value[:, H:], passes)
    circulant_dots(ops, prop, acc, "right", passes)
    for start in range(0, H, STEP):
        upper, lower = pl.ds(start, STEP), pl.ds(H + start, STEP)
        for source, target in ((left_half, upper), (right_half, lower)):
            plus_upper, minus_upper = acc[0, upper, source], acc[1, upper, source]
            plus_lower, minus_lower = acc[0, lower, source], acc[1, lower, source]
            for cols, top, bottom in (
                (left_half, plus_upper + minus_upper, plus_lower + minus_lower),
                (right_half, plus_upper - minus_upper, plus_lower - minus_lower),
            ):
                set_parts(ops, 0, target, cols, top + bottom, passes)
                set_parts(ops, 1, target, cols, top - bottom, passes)
    circulant_dots(ops, prop, acc, "left", passes)


def propagated(acc, start, conj):
    inner = start % H
    real, imag = (
        acc[0, pl.ds(row, STEP), :] + acc[1, pl.ds(row, STEP), :]
        if start < H
        else acc[0, pl.ds(row, STEP), :] - acc[1, pl.ds(row, STEP), :]
        for row in (inner, H + inner)
    )
    return real, -imag if conj else imag


def iota(dim):
    return lax.broadcasted_iota(jnp.int32, (STEP, W), dim)


def windowed(full, part, rows, col):
    return jnp.where(iota(1) >= col, full[part, rows, :W], full[part, rows, W:])


def at_core():
    return lax.axis_index("cuts")


def spread(offsets, which):
    return jnp.broadcast_to(offsets[0:1, which : which + 1], (STEP, W))


def encode_kernel(offsets, live, own, coded):
    col = spread(offsets, 1)
    held = own.at[:, 0]
    peak = jnp.zeros((8, W), jnp.float32)
    for start in range(0, W, STEP):
        rows = pl.ds(start, STEP)
        real, imag = windowed(held, 0, rows, col), windowed(held, 1, rows, col)
        high = jnp.maximum(jnp.abs(real), jnp.abs(imag))
        for piece in range(0, STEP, 8):
            peak = jnp.maximum(peak, high[piece : piece + 8])
    peak = jnp.max(jnp.max(peak, axis=1, keepdims=True), axis=0, keepdims=True)
    peak = jnp.broadcast_to(jnp.maximum(peak, 1e-30), (1, W))
    power = jnp.ceil(jnp.log(peak) * (1.0 / math.log(2.0)))
    gain = jnp.exp2(-power) * TOP
    for part in range(2):
        for start in range(0, W, STEP):
            rows = pl.ds(start, STEP)
            scaled = jnp.round(windowed(held, part, rows, col) * gain)
            coded[part, rows, :] = scaled.astype(jnp.int32).astype(jnp.int16)
    flag = jnp.where(live[0] > 0, 1, 0)
    coded[0, pl.ds(W, HEAD), :] = jnp.broadcast_to(power.astype(jnp.int32), (HEAD, W)).astype(jnp.int16)
    coded[1, pl.ds(W, HEAD), :] = jnp.full((HEAD, W), flag, jnp.int32).astype(jnp.int16)


def mixed_kernel(before, live, own, measured, coded, mixed):
    encode_kernel(before, live, own, coded)

    @pl.when(at_core() == 0)
    def _():
        for start in range(0, W, STEP):
            rows = pl.ds(start, STEP)
            scaled = jnp.round(measured[0, rows, :] * (1.0 / MEASURED_STEP))
            mixed[0, rows, :] = scaled.astype(jnp.int32).astype(jnp.int16)

    @pl.when(at_core() != 0)
    def _():
        mixed[...] = coded[...]


def head_of(coded, part):
    return coded[part, pl.ds(W, HEAD), :].astype(jnp.int32).astype(jnp.float32)[0:1]


def gain_of(coded):
    return jnp.exp2(head_of(coded, 0)) * (1.0 / TOP)


def decoded(coded, part, rows, gain):
    return coded[part, rows, :].astype(jnp.int32).astype(jnp.float32) * gain


def roll_kernel(offsets, before, illumination, rolled):
    row = lax.rem(jnp.where(at_core() == 0, before[0, 0], offsets[0, 0]), W)
    col = lax.rem(jnp.where(at_core() == 0, before[0, 1], offsets[0, 1]), W)
    for part in range(2):
        rolled[part] = pltpu.roll(pltpu.roll(illumination[part], row, 0), col, 1)


def multiplied(wave, patch):
    def rows_of(rows, start):
        wave_real, wave_imag = wave[0, rows, :].astype(jnp.float32), wave[1, rows, :].astype(jnp.float32)
        patch_real, patch_imag = patch(0, rows, start), patch(1, rows, start)
        return wave_real * patch_real - wave_imag * patch_imag, wave_real * patch_imag + wave_imag * patch_real

    return rows_of


def times_patch(wave, patch, out):
    product_of = multiplied(wave, patch)
    for start in range(0, W, STEP):
        rows = pl.ds(start, STEP)
        out[0, rows, :], out[1, rows, :] = product_of(rows, start)


def chosen(row, upper, lower):
    return lambda part, rows, start: jnp.where(
        start + iota(0) >= row, lower(part, rows), upper(part, rows)
    )


def first_slice(rolled, patch, prop, psi, ops, acc):
    propagate(multiplied(rolled, patch), prop, ops, acc, 3, False)
    for start in range(0, W, STEP):
        rows = pl.ds(start, STEP)
        real, imag = propagated(acc, start, False)
        psi[0, rows, :] = real.astype(jnp.bfloat16)
        psi[1, rows, :] = imag.astype(jnp.bfloat16)


def first_kernel(offsets, before, direct, own, rolled, prop, psi, ops, acc):
    @pl.when(at_core() == 0)
    def _():
        gain = gain_of(direct)
        local = own.at[:, 0]
        col = spread(before, 1)
        patch = chosen(
            spread(before, 0),
            lambda part, rows: windowed(local, part, rows, col),
            lambda part, rows: decoded(direct, part, rows, gain),
        )
        first_slice(rolled, patch, prop, psi, ops, acc)


def keeping(given, patch):
    def kept(part, rows, start):
        value = given(part, rows, start)
        patch[part, rows, :] = value
        return value

    return kept


def second_slice(given, psi, far, patch, field, chi):
    times_patch(psi, keeping(given, patch), chi)
    out_real, out_imag = transform(chi[0], chi[1], far, False)
    field[0] = out_real
    field[1] = out_imag


def second_kernel(offsets, before, crossed, edge, rolled, early, prop, far, psi, patch, field, chi, ops, acc):
    row = jnp.where(at_core() == 0, spread(before, 0), spread(offsets, 0))
    gain_crossed, gain_edge = gain_of(crossed), gain_of(edge)
    given = chosen(
        row,
        lambda part, rows: decoded(edge, part, rows, gain_edge),
        lambda part, rows: decoded(crossed, part, rows, gain_crossed),
    )

    @pl.when(at_core() == 0)
    def _():
        psi[...] = early[...]
        second_slice(given, psi, far, patch, field, chi)

    @pl.when(at_core() != 0)
    def _():
        first_slice(rolled, given, prop, psi, ops, acc)


def conj_times(first, real, imag, out):
    for start in range(0, W, STEP):
        rows = pl.ds(start, STEP)
        keep = slice(start, start + STEP)
        first_real, first_imag = first[0, rows, :].astype(jnp.float32), first[1, rows, :].astype(jnp.float32)
        out[0, rows, :] = (first_real * real[keep] + first_imag * imag[keep]).astype(out.dtype)
        out[1, rows, :] = (first_real * imag[keep] - first_imag * real[keep]).astype(out.dtype)


def last_slice(half, rolled, prop, out, ops, acc):
    propagate(
        lambda rows, start: (half[0, rows, :].astype(jnp.float32), half[1, rows, :].astype(jnp.float32)),
        prop,
        ops,
        acc,
        LAST_PASSES,
        True,
    )
    for start in range(0, W, STEP):
        rows = pl.ds(start, STEP)
        real, imag = propagated(acc, start, True)
        wave_real, wave_imag = rolled[0, rows, :], rolled[1, rows, :]
        out[0, rows, :] = (wave_real * real + wave_imag * imag).astype(out.dtype)
        out[1, rows, :] = (wave_real * imag - wave_imag * real).astype(out.dtype)


def third_kernel(
    offsets, live, direct, border, own, measured, field, psi, patch, rolled, prop, far, send, early, half,
    chi, late_patch, late_field, ops, acc,
):
    @pl.when(at_core() != 0)
    def _():
        gain_border = gain_of(border)
        local = own.at[:, 0]
        col = spread(offsets, 1)
        last = chosen(
            spread(offsets, 0),
            lambda part, rows: decoded(border, part, rows, gain_border),
            lambda part, rows: windowed(local, part, rows, col),
        )
        second_slice(last, psi, far, late_patch, late_field, chi)

    def residue(field, target, alive):
        for start in range(0, W, STEP):
            rows = pl.ds(start, STEP)
            real, imag = field[0, rows, :], field[1, rows, :]
            weight = (real * real + imag * imag - target(rows)) * alive
            chi[0, rows, :] = weight * real
            chi[1, rows, :] = weight * imag

    @pl.when(at_core() == 0)
    def _():
        head = head_of(direct, 1)
        residue(field, lambda rows: border[0, rows, :].astype(jnp.int32).astype(jnp.float32) * MEASURED_STEP, head)

    @pl.when(at_core() != 0)
    def _():
        residue(late_field, lambda rows: measured[0, rows, :], jnp.where(live[0] > 0, 1.0, 0.0))

    real, imag = transform(chi[0], chi[1], far, True)

    @pl.when(at_core() == 0)
    def _():
        conj_times(patch, real, imag, half)
        conj_times(psi, real, imag, send)

    @pl.when(at_core() != 0)
    def _():
        conj_times(late_patch, real, imag, half)
        conj_times(psi, real, imag, early)
        last_slice(half, rolled, prop, send, ops, acc)


def fourth_kernel(half, rolled, early, prop, stay, ops, acc):
    @pl.when(at_core() == 0)
    def _():
        last_slice(half, rolled, prop, stay, ops, acc)

    @pl.when(at_core() != 0)
    def _():
        stay[...] = early[...]


def place_kernel(offsets, before, stay, came, out, staged, sems):
    row, col = spread(offsets, 0), spread(offsets, 1)
    row_before, col_before = spread(before, 0), spread(before, 1)

    def place(own, spill):
        copies = []
        for index, start in enumerate(range(0, W, FLUSH)):
            for inner in range(start, start + FLUSH, STEP):
                rows = pl.ds(inner, STEP)
                for part in range(2):
                    mine = jnp.where(inner + iota(0) >= row, own[part, rows, :].astype(jnp.float32), 0.0)
                    theirs = jnp.where(inner + iota(0) < row_before, spill[part, rows, :].astype(jnp.float32), 0.0)
                    here, there = iota(1) >= col, iota(1) >= col_before
                    staged[part, 0, rows, :W] = jnp.where(here, mine, 0.0) + jnp.where(there, theirs, 0.0)
                    staged[part, 0, rows, W:] = jnp.where(here, 0.0, mine) + jnp.where(there, 0.0, theirs)
            block = (slice(None), slice(None), pl.ds(start, FLUSH))
            copies.append(pltpu.make_async_copy(staged.at[block], out.at[block], sems.at[index]))
            copies[-1].start()
        for copy in copies:
            copy.wait()

    @pl.when(at_core() == 0)
    def _():
        place(came, stay)

    @pl.when(at_core() != 0)
    def _():
        place(stay, came)


def call(kernel, outs, specs, scratch=(), out_spec=VMEM, mib=16):
    return pl.pallas_call(
        kernel,
        out_shape=outs,
        in_specs=[{"s": SMEM, "v": VMEM, "a": ANY}[s] for s in specs],
        out_specs=jax.tree.map(lambda _: out_spec, outs),
        scratch_shapes=scratch,
        compiler_params=pltpu.CompilerParams(vmem_limit_bytes=mib << 20),
    )


def shaped(shape, dtype):
    return jax.ShapeDtypeStruct(shape, dtype)


WAVE = shaped((2, W, W), jnp.float32)
HALF_WAVE = shaped((2, W, W), jnp.bfloat16)
CODED = shaped((2, W + HEAD, W), jnp.int16)
CHI = pltpu.VMEM((2, W, W), jnp.float32)
PROPAGATE = [pltpu.VMEM((4, W, W), jnp.bfloat16), pltpu.VMEM((2, W, W), jnp.float32)]


def on_device(transmission, illumination, measured, offsets, live_count):
    prop, far = (jnp.asarray(t) for t in tables())
    count = lax.axis_size("tile")

    def permute(value, target):
        pairs = []
        for c in range(2):
            for k in range(count):
                to_core, to_tile = target(c, k)
                pairs.append((c * count + k, to_core * count + to_tile % count))
        return lax.ppermute(value, ("cuts", "tile"), pairs)

    before = permute(offsets, lambda c, k: (c, k + 1))
    place = (offsets, before)
    encode = call(encode_kernel, CODED, "vsv")
    ahead = encode(offsets, live_count, transmission)
    direct = permute(ahead, lambda c, k: (0, k + 1) if c == 0 else (1, k ^ ASIDE))
    behind, mixed = call(mixed_kernel, (CODED, CODED), "vsvv")(
        before, live_count, transmission, measured
    )
    crossed = permute(ahead, lambda c, k: (1, k) if c == 0 else (0, k + 1))
    border = permute(mixed, lambda c, k: (0, k + 1) if c == 0 else (1, k - 1))
    edge = permute(behind, lambda c, k: (1, k - 1) if c == 0 else (0, k))
    rolled = call(roll_kernel, WAVE, "ssv")(*place, illumination)
    early = call(first_kernel, HALF_WAVE, "vvvvvv", PROPAGATE)(*place, direct, transmission, rolled, prop)
    psi, patch, field = call(second_kernel, (HALF_WAVE, WAVE, WAVE), "v" * 8, [CHI, *PROPAGATE])(
        *place, crossed, edge, rolled, early, prop, far
    )
    send, early_stay, half = call(
        third_kernel, (HALF_WAVE, HALF_WAVE, HALF_WAVE), "vs" + "v" * 10, [CHI, CHI, CHI, *PROPAGATE]
    )(offsets, live_count, direct, border, transmission, measured, field, psi, patch, rolled, prop, far)
    came = permute(send, lambda c, k: (1 - c, k))
    stay = call(fourth_kernel, HALF_WAVE, "vvvv", PROPAGATE)(half, rolled, early_stay, prop)
    return call(
        place_kernel,
        shaped(transmission.shape, jnp.float32),
        "vvvv",
        [pltpu.VMEM(transmission.shape, jnp.float32), pltpu.SemaphoreType.DMA((W // FLUSH,))],
        ANY,
    )(*place, stay, came)


def solution(mesh):
    placed = (P(None, "cuts", "tile", None), P(), P("tile", None, None), P("tile", None), P("tile"))
    return jax.shard_map(
        on_device,
        mesh=mesh,
        in_specs=placed,
        out_specs=P(None, "cuts", "tile", None),
        check_vma=False,
    )
```
